32 devices in a mesh: groups: 2 (over x), step: 2 (over core), person: 8 (over z, y).
Axes of the slice: x: 2, y: 2, z: 4, core: 2. Of those that a mesh axis runs over, the one named last changes fastest.
Arguments:
- chain: float32 [8, 128, 4, 512], P(('groups', 'step'), 'person'), parts along dimension 0, may hold values from -6 to 6
- start: float32 [256, 4, 512], P(('groups', 'person')), parts along dimension 0, may hold values from -6 to 6
- noise: bfloat16 [8, 128, 4, 512], P(('groups', 'step'), 'person'), parts along dimension 0, may hold values from -6 to 6
- timesteps: int32 [8], P(('groups', 'step')), parts along dimension 0, may hold values from 1 to 1000
- rates: float32 [8], P(('groups', 'step')), parts along dimension 0, may hold values from 0.05 to 0.5
- noise_scales: float32 [8], P(('groups', 'step')), parts along dimension 0, may hold values from 0.1 to 0.5
- time_weight: bfloat16 [512, 512], replicated, may hold values from -0.25 to 0.25
- w_query: bfloat16 [2, 512, 512], replicated, may hold values from -1.75 to 1.75
- w_keyval: bfloat16 [2, 512, 1024], replicated, may hold values from -0.25 to 0.25
- w_attn_out: bfloat16 [2, 512, 512], replicated, may hold values from -0.25 to 0.25
- w_up: bfloat16 [2, 512, 1024], replicated, may hold values from -0.25 to 0.25
- w_down: bfloat16 [2, 1024, 512], replicated, may hold values from -0.1875 to 0.1875
- gains: float32 [2, 2, 512], replicated, may hold values from 0.1 to 1.9
- final_gain: float32 [512], replicated, may hold values from 0.1 to 1.9
- w_output: bfloat16 [512, 512], replicated, may hold values from -0.25 to 0.25
Outputs:
- new_chain: float32 [8, 128, 4, 512], P(('groups', 'step'), 'person'), parts along dimension 0
The draws below stay inside these ranges and needn't reach their ends.
There are 2 independent parts, one for each index of `groups`. The reference program is written for one: setup_inputs(seed, part) draws one part's arguments, and reference() takes and returns one part's arrays. A program takes and returns all parts, laid end to end along the dimension named above; an argument that names none is the same for every part. Nothing has to cross between parts.
All inputs are finite; a program needn't handle non-finite values.
Results may differ from the reference program's by a relative error of at most 0.004.
Values may be sent and summed in bfloat16 or wider, within the bound.
A program may use at most 64 MiB of HBM per device.

```python
import math
import jax
import jax.numpy as jnp
from jax import lax

D = 512
HEADS = 8
FFN = 1024
L = 4
LAYERS = 2
TSTEPS = 1000
S = 4
P_SIZE = 128
KEYS = 512


def set_ends(entries, rng, low, top_value):
    longest = entries.shape.index(max(entries.shape))
    spots = []
    for shift in (0, 1):
        where = [jax.random.randint(jax.random.fold_in(rng, axis), (), 0, length) for axis, length in enumerate(entries.shape)]
        where[longest] = (where[longest] + shift) % entries.shape[longest]
        spots.append(tuple(where))
    return entries.at[spots[0]].set(low).at[spots[1]].set(top_value)


def shard_levels(own_key, shape, shards, low, largest):
    level, own = 1.0, jax.random.fold_in(own_key, 6)
    for dim, blocks in shards:
        steps = jnp.exp(jax.random.uniform(jax.random.fold_in(own, dim), (blocks,), jnp.float32, low / len(shards), largest / len(shards)))
        level = level * jnp.repeat(steps, shape[dim] // blocks).reshape([-1 if axis == dim else 1 for axis in range(len(shape))])
    return level


def scatter_about(stream_key, dims, deviation, bound, pieces=(), dtype=jnp.bfloat16):
    array = deviation * jax.random.normal(stream_key, dims, jnp.float32)
    if pieces:
        array = array * shard_levels(stream_key, dims, pieces, -0.22, 0.18)
    return jnp.clip(array, -bound, bound).astype(dtype)


def setup_inputs(seed: int = 0, part: int = 0) -> dict:
    keys = jax.random.split(jax.random.key(seed), 16)
    part_splits = jax.random.split(jax.random.fold_in(keys[15], part), 16)
    chain = scatter_about(part_splits[0], (S, P_SIZE, L, D), 1.0, 6.0, ((0, 2), (1, 8)), jnp.float32)
    start = scatter_about(part_splits[1], (P_SIZE, L, D), 1.0, 6.0, ((0, 8),), jnp.float32)
    noise = scatter_about(part_splits[2], (S, P_SIZE, L, D), 1.0, 6.0, ((0, 2), (1, 8)))
    timesteps = set_ends(jax.random.randint(part_splits[3], (S,), 1, TSTEPS + 1), jax.random.fold_in(part_splits[3], 1), 1, TSTEPS).astype(jnp.int32)
    rates = jnp.clip(jnp.exp(math.log(0.5) - 2.3025851 * jax.random.uniform(part_splits[4], (S,), jnp.float32) ** shard_levels(part_splits[4], (S,), ((0, 2),), -0.2, 0.2)), 0.05, 0.5)
    noise_scales = jnp.clip(jnp.exp(math.log(0.5) - 1.609438 * jax.random.uniform(part_splits[5], (S,), jnp.float32) ** shard_levels(part_splits[5], (S,), ((0, 2),), -0.2, 0.2)), 0.1, 0.5)
    time_weight = scatter_about(keys[6], (D, D), D ** -0.5, 0.25)
    w_query = scatter_about(keys[7], (LAYERS, D, D), (2.5 / D ** 0.5), 1.75)
    w_keyval = scatter_about(keys[8], (LAYERS, D, 2 * D), D ** -0.5, 0.25)
    w_attn_out = scatter_about(keys[9], (LAYERS, D, D), D ** -0.5, 0.25)
    w_up = scatter_about(keys[10], (LAYERS, D, FFN), D ** -0.5, 0.25)
    w_down = scatter_about(keys[11], (LAYERS, FFN, D), FFN ** -0.5, 0.1875)
    gains = jnp.clip(1.0 + 0.18 * jax.random.normal(keys[12], (LAYERS, 2, D), jnp.float32), 0.1, 1.9)
    final_gain = jnp.clip(1.0 + 0.18 * jax.random.normal(keys[13], (D,), jnp.float32), 0.1, 1.9)
    w_output = scatter_about(keys[14], (D, D), D ** -0.5, 0.25)
    return {"chain": chain, "start": start, "noise": noise, "timesteps": timesteps, "rates": rates, "noise_scales": noise_scales, "time_weight": time_weight, "w_query": w_query, "w_keyval": w_keyval, "w_attn_out": w_attn_out, "w_up": w_up, "w_down": w_down, "gains": gains, "final_gain": final_gain, "w_output": w_output}


def time_features(timesteps, feature_width):
    half_width = feature_width // 2
    freqs = jnp.exp(-math.log(10000.0) * jnp.arange(half_width).astype(jnp.float32) / half_width)
    angles = timesteps.astype(jnp.float32)[:, None] * freqs[None, :]
    return jnp.concatenate([jnp.sin(angles), jnp.cos(angles)], axis=1)

def rms_norm(values, gain):
    return values * lax.rsqrt(lax.optimization_barrier(jnp.mean(values * values, axis=-1, keepdims=True)) + 1e-06) * gain

def reference(chain, start, noise, timesteps, rates, noise_scales, time_weight, w_query, w_keyval, w_attn_out, w_up, w_down, gains, final_gain, w_output):
    window = chain.shape[0]
    head_dim = D // HEADS
    points = jnp.concatenate([start[None], chain[:-1]], axis=0).reshape(window, KEYS, D)
    embedded = time_features(timesteps, D).astype(jnp.bfloat16)
    temb = jax.nn.silu(jnp.dot(embedded, time_weight, preferred_element_type=jnp.float32))

    def denoise(packed):
        hidden, time_row = packed
        hidden = hidden + time_row[None, :]
        for layer_index in range(LAYERS):
            normed = rms_norm(hidden, gains[layer_index, 0]).astype(jnp.bfloat16)
            queries = jnp.dot(normed, w_query[layer_index], preferred_element_type=jnp.float32).astype(jnp.bfloat16)
            keyval = jnp.dot(normed, w_keyval[layer_index], preferred_element_type=jnp.float32).astype(jnp.bfloat16)
            q_heads = queries.reshape(KEYS, HEADS, head_dim).astype(jnp.float32)
            k_heads = keyval[:, :D].reshape(KEYS, HEADS, head_dim).astype(jnp.float32)
            v_heads = keyval[:, D:].reshape(KEYS, HEADS, head_dim).astype(jnp.float32)
            scores = jnp.einsum('qhd,khd->hqk', q_heads, k_heads) / math.sqrt(head_dim)
            expo = jnp.exp(30.0 * jnp.tanh(scores / 30.0))
            weights = (expo / lax.optimization_barrier(jnp.sum(expo, axis=-1, keepdims=True))).astype(jnp.bfloat16)
            attended = jnp.einsum('hqk,khd->qhd', weights.astype(jnp.float32), v_heads).reshape(KEYS, D).astype(jnp.bfloat16)
            hidden = hidden + jnp.dot(attended, w_attn_out[layer_index], preferred_element_type=jnp.float32)
            mixed = rms_norm(hidden, gains[layer_index, 1]).astype(jnp.bfloat16)
            upward = jax.nn.gelu(jnp.dot(mixed, w_up[layer_index], preferred_element_type=jnp.float32)).astype(jnp.bfloat16)
            hidden = hidden + jnp.dot(upward, w_down[layer_index], preferred_element_type=jnp.float32)
        final_rows = rms_norm(hidden, final_gain).astype(jnp.bfloat16)
        return jnp.dot(final_rows, w_output, preferred_element_type=jnp.float32)
    predicted = lax.map(denoise, (points, temb))
    drift = rates[:, None, None] * (predicted - points) + noise_scales[:, None, None] * noise.reshape(window, KEYS, D).astype(jnp.float32)
    new_chain = start.reshape(KEYS, D)[None] + jnp.cumsum(drift, axis=0)
    return new_chain.reshape(window, P_SIZE, L, D)
```

```python
import functools
import math

import jax
import jax.numpy as jnp
from jax import lax
from jax.experimental import pallas as pl
from jax.experimental.pallas import tpu as pltpu
from jax.sharding import PartitionSpec as P

HEADS = 8
MESH = pl.DeviceIdType.MESH
BF = jnp.bfloat16
F32 = jnp.float32


def dot(a, b):
    return jnp.dot(a, b, preferred_element_type=F32)


def rms_norm(values, gain):
    return values * lax.rsqrt(jnp.mean(values * values, axis=-1, keepdims=True) + 1e-06) * gain


def kernel(
    sizes,
    chain_ref, start_ref, noise_ref, times_ref, rates_ref, scales_ref,
    tw_ref, wq_ref, wkv_ref, wo_ref, wu_ref, wd_ref, gains_ref, fgain_ref, wout_ref,
    out_ref,
    chain_v, start_v, noise_v, tw_v, wq_v, wkv_v, wo_v, wu_v, wd_v, wout_v,
    send_v, recv_v, temb_v, prev_v, gath, pout, pin, tot_out, tot_in,
    load_sem, ssend, srecv, tsend, trecv, vsend, vrecv, gsend, grecv, nsend, nrecv, fsend, frecv,
    rsend, rrecv, usend, urecv,
):
    n, cores, h, rows, width, layers = sizes
    window = h * cores
    teams = n // window
    mine = h * rows
    me_p, me_s = lax.axis_index("person"), lax.axis_index("step")
    spot, j = me_p // teams, me_p % teams

    def device(person, step):
        return {"person": person, "step": step}

    def remote(src, dst, send_sem, recv_sem, person, step):
        return pltpu.make_async_remote_copy(
            src_ref=src, dst_ref=dst, send_sem=send_sem, recv_sem=recv_sem,
            device_id=device(person, step), device_id_type=MESH,
        )

    loads = {}

    def load(name, src, dst):
        copy = pltpu.make_async_copy(src, dst, load_sem.at[len(loads)])
        loads[name] = copy
        copy.start()

    load("chain", chain_ref, chain_v)
    load("start", start_ref, start_v)
    load("tw", tw_ref, tw_v)
    for l in range(layers):
        load(("wq", l), wq_ref.at[l], wq_v.at[l])
        load(("wkv", l), wkv_ref.at[l], wkv_v.at[l])
        load(("wo", l), wo_ref.at[l], wo_v.at[l])
        load(("wu", l), wu_ref.at[l], wu_v.at[l])
        load(("wd", l), wd_ref.at[l], wd_v.at[l])
    load("wout", wout_ref, wout_v)
    load("noise", noise_ref, noise_v)

    barrier = pltpu.get_barrier_semaphore()
    for dq in range(window):
        for ds in range(cores):
            if dq or ds:
                pl.semaphore_signal(
                    barrier, inc=1,
                    device_id=device(((spot + dq) % window) * teams + j, (me_s + ds) % cores),
                    device_id_type=MESH,
                )
    for d in range(1, teams):
        pl.semaphore_signal(
            barrier, inc=1, device_id=device(spot * teams + (j + d) % teams, me_s), device_id_type=MESH
        )

    loads["chain"].wait()
    loads["start"].wait()
    is_last = me_s == cores - 1
    for t in range(h):
        block = chain_v[t].reshape(rows, width)
        if t == h - 1:
            block = jnp.where(is_last, start_v[...].reshape(rows, width), block)
        send_v[t] = block.astype(BF)
    pl.semaphore_wait(barrier, window * cores - 1 + teams - 1)

    scatter = []
    for t in range(h):
        position = (me_s * h + t + 1) % window
        to_p, to_s, slot = position * teams + j, spot // h, spot % h
        own = (to_p == me_p) & (to_s == me_s)
        copy = remote(send_v.at[t], recv_v.at[slot], ssend.at[t], srecv.at[slot], to_p, to_s)
        scatter.append((own, copy))

        @pl.when(jnp.logical_not(own))
        def _():
            copy.start()

        @pl.when(own)
        def _():
            recv_v[slot] = send_v[t]

    hand = remote(chain_v.at[h - 1], prev_v, vsend.at[0], vrecv.at[0], me_p, (me_s + 1) % cores)

    @pl.when(me_s < cores - 1)
    def _():
        hand.start()

    lane = lax.broadcasted_iota(jnp.int32, (8, width), 1)
    sub = lax.broadcasted_iota(jnp.int32, (8, width), 0)
    half = width // 2
    index = jnp.where(lane < half, lane, lane - half).astype(F32)
    freqs = jnp.exp(-math.log(10000.0) * index / half)
    when = jnp.zeros((8, width), F32)
    for t in range(h):
        when = jnp.where(sub == t, times_ref[t].astype(F32), when)
    angles = when * freqs
    features = jnp.where(lane < half, jnp.sin(angles), jnp.cos(angles)).astype(BF)
    loads["tw"].wait()
    temb = dot(features, tw_v[...])
    temb_v[me_s] = temb * (1.0 / (1.0 + jnp.exp(-temb)))
    shares = []
    for d in range(1, cores):
        share = remote(
            temb_v.at[me_s], temb_v.at[me_s], tsend.at[d - 1], trecv.at[d - 1], me_p, (me_s + d) % cores
        )
        share.start()
        shares.append(share)
    for d in range(1, cores):
        other = (me_s + cores - d) % cores
        remote(temb_v.at[other], temb_v.at[other], tsend.at[d - 1], trecv.at[d - 1], me_p, other).wait_recv()
    time_row = temb_v[spot // h, pl.ds(spot % h, 1), :]

    from_s = ((spot + window - 1) % window) // h
    for b in range(h):
        own = (me_s * h + b == spot) & (from_s == me_s)

        @pl.when(jnp.logical_not(own))
        def _():
            remote(
                recv_v.at[b], recv_v.at[b], ssend.at[0], srecv.at[b], me_p, (me_s + 1) % cores
            ).wait_recv()

    hidden = recv_v[...].reshape(mine, width).astype(F32) + time_row

    head_dim = width // HEADS
    wide = min(256, width)
    per = wide // head_dim
    groups = width // wide
    lane_head = lax.broadcasted_iota(jnp.int32, (mine, wide), 1) // head_dim
    masks = [lane_head == i for i in range(per)]
    inner = 1.0 / (math.sqrt(head_dim) * 30.0)
    outer = 30.0 * math.log2(math.e)
    sends = []

    for l in range(layers):
        normed = rms_norm(hidden, gains_ref[2 * l : 2 * l + 1, :]).astype(BF)
        gath[l, j, me_s] = normed
        own_block = gath.at[l, j, me_s]
        for d in range(1, teams):
            copy = remote(
                own_block, own_block, gsend.at[l, d - 1], grecv.at[l, d - 1],
                spot * teams + (j + d) % teams, me_s,
            )
            copy.start()
            sends.append(copy)
        for e in range(1, cores):
            copy = remote(
                own_block, own_block, nsend.at[l, e - 1], nrecv.at[l, e - 1], me_p, (me_s + e) % cores
            )
            copy.start()
            sends.append(copy)
        loads["wq", l].wait()
        queries = dot(normed, wq_v[l]).astype(BF)
        stacked = []
        for g in range(groups):
            piece = queries[:, g * wide : (g + 1) * wide]
            stacked.append(jnp.concatenate([jnp.where(m, piece, jnp.zeros_like(piece)) for m in masks], axis=0))
        loads["wkv", l].wait()

        def round_of(team, carry, l=l, stacked=stacked):
            sums, dens = carry
            keyval = dot(gath[l, team].reshape(cores * mine, width), wkv_v[l]).astype(BF)
            new_sums, new_dens = [], []
            for g in range(groups):
                keys = keyval[:, g * wide : (g + 1) * wide]
                values = keyval[:, width + g * wide : width + (g + 1) * wide]
                scores = lax.dot_general(
                    stacked[g], keys, (((1,), (1,)), ((), ())), preferred_element_type=F32
                )
                expo = jnp.exp2(jnp.tanh(scores * inner) * outer)
                part = dot(expo.astype(BF), values)
                total = sums[g]
                for i in range(per):
                    total = total + jnp.where(masks[i], part[i * mine : (i + 1) * mine], 0.0)
                new_sums.append(total)
                den = dens[g]
                for c in range(0, cores * mine, 128):
                    den = den + expo[:, c : c + 128]
                new_dens.append(den)
            return tuple(new_sums), tuple(new_dens)

        carry = (
            tuple(jnp.zeros((mine, wide), F32) for _ in range(groups)),
            tuple(jnp.zeros((per * mine, 128), F32) for _ in range(groups)),
        )
        for e in range(1, cores):
            other = gath.at[l, j, (me_s + cores - e) % cores]
            remote(
                other, other, nsend.at[l, e - 1], nrecv.at[l, e - 1], me_p, (me_s + e) % cores
            ).wait_recv()
        carry = round_of(j, carry)
        for d in range(1, teams):
            team = (j + teams - d) % teams
            block = gath.at[l, team, me_s]
            remote(
                block, block, gsend.at[l, d - 1], grecv.at[l, d - 1], spot * teams + team, me_s
            ).wait_recv()
            for e in range(1, cores):
                copy = remote(
                    block, block, fsend.at[l, d - 1, e - 1], frecv.at[l, d - 1, e - 1],
                    me_p, (me_s + e) % cores,
                )
                copy.start()
                sends.append(copy)
        for d in range(1, teams):
            team = (j + teams - d) % teams
            for e in range(1, cores):
                block = gath.at[l, team, (me_s + cores - e) % cores]
                remote(
                    block, block, fsend.at[l, d - 1, e - 1], frecv.at[l, d - 1, e - 1],
                    me_p, (me_s + e) % cores,
                ).wait_recv()
        if teams <= 2:
            for d in range(1, teams):
                carry = round_of((j + teams - d) % teams, carry)
        else:
            carry = lax.fori_loop(1, teams, lambda d, c: round_of((j + teams - d) % teams, c), carry)
        sums, dens = carry
        pieces = []
        for g in range(groups):
            inverse = 1.0 / jnp.sum(dens[g], axis=-1, keepdims=True)
            scale = jnp.zeros((mine, wide), F32)
            for i in range(per):
                scale = jnp.where(masks[i], inverse[i * mine : (i + 1) * mine], scale)
            pieces.append((sums[g] * scale).astype(BF))
        attended = jnp.concatenate(pieces, axis=1)
        loads["wo", l].wait()
        hidden = hidden + dot(attended, wo_v[l])
        mixed = rms_norm(hidden, gains_ref[2 * l + 1 : 2 * l + 2, :]).astype(BF)
        loads["wu", l].wait()
        upward = jax.nn.gelu(dot(mixed, wu_v[l])).astype(BF)
        loads["wd", l].wait()
        hidden = hidden + dot(upward, wd_v[l])

    final_rows = rms_norm(hidden, fgain_ref[...]).astype(BF)
    loads["wout"].wait()
    predicted = dot(final_rows, wout_v[...]).astype(BF)

    returns = []
    for b in range(h):
        pout[b] = predicted[b * rows : (b + 1) * rows]
        to_p, to_s, slot = (me_s * h + b) * teams + j, spot // h, spot % h
        own = (to_p == me_p) & (to_s == me_s)
        copy = remote(pout.at[b], pin.at[slot], rsend.at[b], rrecv.at[slot], to_p, to_s)
        returns.append((own, copy))

        @pl.when(jnp.logical_not(own))
        def _():
            copy.start()

        @pl.when(own)
        def _():
            pin[slot] = pout[b]

    @pl.when(me_s > 0)
    def _():
        remote(prev_v, prev_v, vsend.at[0], vrecv.at[0], me_p, (me_s + 1) % cores).wait_recv()

    @pl.when(me_s == 0)
    def _():
        prev_v[...] = start_v[...]

    loads["noise"].wait()
    first = start_v[...].reshape(rows, width)
    bases = []
    total = jnp.zeros((rows, width), F32)
    for t in range(h):
        points = (prev_v[...] if t == 0 else chain_v[t - 1]).reshape(rows, width)
        noise = noise_v[t].astype(F32).reshape(rows, width)
        total = total + (scales_ref[t] * noise - rates_ref[t] * points)
        bases.append(total)
    running = jnp.zeros((rows, width), F32)
    sums = []
    for t in range(h):
        own = ((me_s * h + t) * teams + j == me_p) & (spot // h == me_s)

        @pl.when(jnp.logical_not(own))
        def _():
            remote(
                pin.at[t], pin.at[t], rsend.at[0], rrecv.at[t], me_p, (me_s + 1) % cores
            ).wait_recv()

        running = running + rates_ref[t] * pin[t].astype(F32)
        sums.append(bases[t] + running)
    tot_out[...] = sums[-1]
    ups = []
    for d in range(1, cores):
        up = remote(tot_out, tot_in.at[d - 1], usend.at[d - 1], urecv.at[d - 1], me_p, (me_s + d) % cores)
        ups.append(up)

        @pl.when(me_s + d < cores)
        def _():
            up.start()

    for d in range(1, cores):

        @pl.when(me_s - d >= 0)
        def _():
            remote(
                tot_in.at[d - 1], tot_in.at[d - 1], usend.at[d - 1], urecv.at[d - 1],
                me_p, (me_s + cores - d) % cores,
            ).wait_recv()

    before = first
    for d in range(1, cores):
        before = before + jnp.where(me_s - d >= 0, tot_in[d - 1], 0.0)
    for t in range(h):
        out_ref[t] = (before + sums[t]).reshape(out_ref.shape[1:])

    for own, copy in scatter + returns:

        @pl.when(jnp.logical_not(own))
        def _():
            copy.wait_send()

    @pl.when(me_s < cores - 1)
    def _():
        hand.wait_send()

    for copy in shares + sends:
        copy.wait_send()
    for d, up in enumerate(ups):

        @pl.when(me_s + d + 1 < cores)
        def _():
            up.wait_send()


def local(n, cores, chain, start, noise, timesteps, rates, noise_scales, time_weight, w_query, w_keyval,
          w_attn_out, w_up, w_down, gains, final_gain, w_output):
    h, persons, tokens, width = chain.shape
    rows = persons * tokens
    layers = w_query.shape[0]
    teams = n // (h * cores)
    mine = h * rows
    sizes = (n, cores, h, rows, width, layers)
    any_spec = pl.BlockSpec(memory_space=pl.ANY)
    smem = pl.BlockSpec(memory_space=pltpu.SMEM)
    vmem = pl.BlockSpec(memory_space=pltpu.VMEM)
    dma = pltpu.SemaphoreType.DMA
    peers, teamed = max(cores - 1, 1), max(teams - 1, 1)
    scratch = [
        pltpu.VMEM(chain.shape, F32), pltpu.VMEM(start.shape, F32), pltpu.VMEM(noise.shape, BF),
        pltpu.VMEM(time_weight.shape, BF), pltpu.VMEM(w_query.shape, BF), pltpu.VMEM(w_keyval.shape, BF),
        pltpu.VMEM(w_attn_out.shape, BF), pltpu.VMEM(w_up.shape, BF), pltpu.VMEM(w_down.shape, BF),
        pltpu.VMEM(w_output.shape, BF),
        pltpu.VMEM((h, rows, width), BF), pltpu.VMEM((h, rows, width), BF),
        pltpu.VMEM((cores, 8, width), F32), pltpu.VMEM(start.shape, F32),
        pltpu.VMEM((layers, teams, cores, mine, width), BF),
        pltpu.VMEM((h, rows, width), BF), pltpu.VMEM((h, rows, width), BF),
        pltpu.VMEM((rows, width), F32), pltpu.VMEM((peers, rows, width), F32),
        dma((5 + 5 * layers,)), dma((h,)), dma((h,)), dma((peers,)), dma((peers,)), dma((1,)), dma((1,)),
        dma((layers, teamed)), dma((layers, teamed)), dma((layers, peers)), dma((layers, peers)),
        dma((layers, teamed, peers)), dma((layers, teamed, peers)),
        dma((h,)), dma((h,)), dma((peers,)), dma((peers,)),
    ]
    return pl.pallas_call(
        functools.partial(kernel, sizes),
        out_shape=jax.ShapeDtypeStruct(chain.shape, F32),
        in_specs=[any_spec] * 3 + [smem] * 3 + [any_spec] * 6 + [vmem] * 2 + [any_spec],
        out_specs=vmem,
        scratch_shapes=scratch,
        compiler_params=pltpu.CompilerParams(
            collective_id=0, has_side_effects=True, vmem_limit_bytes=48 * 1024 * 1024
        ),
    )(
        chain, start, noise, timesteps, rates, noise_scales, time_weight, w_query, w_keyval, w_attn_out,
        w_up, w_down, gains.reshape(-1, width), final_gain.reshape(1, width), w_output,
    )


def solution(mesh):
    placed = (
        P(("groups", "step"), "person", None, None),
        P(("groups", "person"), None, None),
        P(("groups", "step"), "person", None, None),
        P(("groups", "step")),
        P(("groups", "step")),
        P(("groups", "step")),
    ) + (P(),) * 9
    return jax.shard_map(
        functools.partial(local, mesh.shape["person"], mesh.shape["step"]),
        mesh=mesh,
        in_specs=placed,
        out_specs=P(("groups", "step"), "person", None, None),
        check_vma=False,
    )
```

```python
import functools
import math

import jax
import jax.numpy as jnp
from jax import lax
from jax.experimental import pallas as pl
from jax.experimental.pallas import tpu as pltpu
from jax.sharding import PartitionSpec as P

HEADS = 8
MESH = pl.DeviceIdType.MESH
BF = jnp.bfloat16
F32 = jnp.float32


def dot(a, b):
    return jnp.dot(a, b, preferred_element_type=F32)


def rms_norm(values, gain):
    return values * lax.rsqrt(jnp.mean(values * values, axis=-1, keepdims=True) + 1e-06) * gain


def kernel(
    sizes,
    chain_ref, start_ref, noise_ref, times_hbm, rates_hbm, scales_hbm,
    tw_ref, wq_ref, wkv_ref, wo_ref, wu_ref, wd_ref, gains_hbm, fgain_hbm, wout_ref,
    out_ref,
    times_ref, rates_ref, scales_ref, gains_ref, fgain_ref, chain_v, start_v, noise_v, tw_v, wq_v, wkv_v, wo_v, wu_v, wd_v, wout_v,
    send_v, recv_v, temb_v, prev_v, gath, pout, pin, tot_out, tot_in,
    load_sem, ssend, srecv, tsend, trecv, vsend, vrecv, gsend, grecv, nsend, nrecv, fsend, frecv,
    rsend, rrecv, usend, urecv,
):
    n, cores, h, rows, width, layers = sizes
    window = h * cores
    teams = n // window
    mine = h * rows
    me_p, me_s = lax.axis_index("person"), lax.axis_index("step")
    spot, j = me_p // teams, me_p % teams

    def device(person, step):
        return {"person": person, "step": step}

    def remote(src, dst, send_sem, recv_sem, person, step):
        return pltpu.make_async_remote_copy(
            src_ref=src, dst_ref=dst, send_sem=send_sem, recv_sem=recv_sem,
            device_id=device(person, step), device_id_type=MESH,
        )

    loads = {}

    def load(name, src, dst):
        copy = pltpu.make_async_copy(src, dst, load_sem.at[len(loads)])
        loads[name] = copy
        copy.start()

    load("chain", chain_ref, chain_v)
    load("start", start_ref, start_v)
    load("times", times_hbm, times_ref)
    load("tw", tw_ref, tw_v)
    load("gains", gains_hbm, gains_ref)
    for l in range(layers):
        load(("wq", l), wq_ref.at[l], wq_v.at[l])
        load(("wkv", l), wkv_ref.at[l], wkv_v.at[l])
        load(("wo", l), wo_ref.at[l], wo_v.at[l])
        load(("wu", l), wu_ref.at[l], wu_v.at[l])
        load(("wd", l), wd_ref.at[l], wd_v.at[l])
    load("wout", wout_ref, wout_v)
    load("noise", noise_ref, noise_v)
    load("fgain", fgain_hbm, fgain_ref)
    load("rates", rates_hbm, rates_ref)
    load("scales", scales_hbm, scales_ref)

    barrier = pltpu.get_barrier_semaphore()
    for dq in range(window):
        for ds in range(cores):
            if dq or ds:
                pl.semaphore_signal(
                    barrier, inc=1,
                    device_id=device(((spot + dq) % window) * teams + j, (me_s + ds) % cores),
                    device_id_type=MESH,
                )
    for d in range(1, teams):
        pl.semaphore_signal(
            barrier, inc=1, device_id=device(spot * teams + (j + d) % teams, me_s), device_id_type=MESH
        )

    loads["chain"].wait()
    loads["start"].wait()
    is_last = me_s == cores - 1
    for t in range(h):
        block = chain_v[t].reshape(rows, width)
        if t == h - 1:
            block = jnp.where(is_last, start_v[...].reshape(rows, width), block)
        send_v[t] = block.astype(BF)
    pl.semaphore_wait(barrier, window * cores - 1 + teams - 1)

    scatter = []
    for t in range(h):
        position = (me_s * h + t + 1) % window
        to_p, to_s, slot = position * teams + j, spot // h, spot % h
        own = (to_p == me_p) & (to_s == me_s)
        copy = remote(send_v.at[t], recv_v.at[slot], ssend.at[t], srecv.at[slot], to_p, to_s)
        scatter.append((own, copy))

        @pl.when(jnp.logical_not(own))
        def _():
            copy.start()

        @pl.when(own)
        def _():
            recv_v[slot] = send_v[t]

    hand = remote(chain_v.at[h - 1], prev_v, vsend.at[0], vrecv.at[0], me_p, (me_s + 1) % cores)

    @pl.when(me_s < cores - 1)
    def _():
        hand.start()

    lane = lax.broadcasted_iota(jnp.int32, (8, width), 1)
    sub = lax.broadcasted_iota(jnp.int32, (8, width), 0)
    half = width // 2
    index = jnp.where(lane < half, lane, lane - half).astype(F32)
    freqs = jnp.exp(-math.log(10000.0) * index / half)
    when = jnp.zeros((8, width), F32)
    loads["times"].wait()
    for t in range(h):
        when = jnp.where(sub == t, times_ref[t].astype(F32), when)
    angles = when * freqs
    features = jnp.where(lane < half, jnp.sin(angles), jnp.cos(angles)).astype(BF)
    loads["tw"].wait()
    temb = dot(features, tw_v[...])
    temb_v[me_s] = temb * (1.0 / (1.0 + jnp.exp(-temb)))
    shares = []
    for d in range(1, cores):
        share = remote(
            temb_v.at[me_s], temb_v.at[me_s], tsend.at[d - 1], trecv.at[d - 1], me_p, (me_s + d) % cores
        )
        share.start()
        shares.append(share)
    for d in range(1, cores):
        other = (me_s + cores - d) % cores
        remote(temb_v.at[other], temb_v.at[other], tsend.at[d - 1], trecv.at[d - 1], me_p, other).wait_recv()
    time_row = temb_v[spot // h, pl.ds(spot % h, 1), :]

    from_s = ((spot + window - 1) % window) // h
    for b in range(h):
        own = (me_s * h + b == spot) & (from_s == me_s)

        @pl.when(jnp.logical_not(own))
        def _():
            remote(
                recv_v.at[b], recv_v.at[b], ssend.at[0], srecv.at[b], me_p, (me_s + 1) % cores
            ).wait_recv()

    hidden = recv_v[...].reshape(mine, width).astype(F32) + time_row

    head_dim = width // HEADS
    wide = min(256, width)
    per = wide // head_dim
    groups = width // wide
    lane_head = lax.broadcasted_iota(jnp.int32, (mine, wide), 1) // head_dim
    masks = [lane_head == i for i in range(per)]
    inner = 1.0 / (math.sqrt(head_dim) * 30.0)
    outer = 30.0 * math.log2(math.e)
    sends = []

    loads["gains"].wait()
    for l in range(layers):
        normed = rms_norm(hidden, gains_ref[l, 0:1, :]).astype(BF)
        gath[l, j, me_s] = normed
        own_block = gath.at[l, j, me_s]
        for d in range(1, teams):
            copy = remote(
                own_block, own_block, gsend.at[l, d - 1], grecv.at[l, d - 1],
                spot * teams + (j + d) % teams, me_s,
            )
            copy.start()
            sends.append(copy)
        for e in range(1, cores):
            copy = remote(
                own_block, own_block, nsend.at[l, e - 1], nrecv.at[l, e - 1], me_p, (me_s + e) % cores
            )
            copy.start()
            sends.append(copy)
        loads["wq", l].wait()
        queries = dot(normed, wq_v[l]).astype(BF)
        stacked = []
        for g in range(groups):
            piece = queries[:, g * wide : (g + 1) * wide]
            stacked.append(jnp.concatenate([jnp.where(m, piece, jnp.zeros_like(piece)) for m in masks], axis=0))
        loads["wkv", l].wait()

        def round_of(team, carry, l=l, stacked=stacked):
            sums, dens = carry
            keyval = dot(gath[l, team].reshape(cores * mine, width), wkv_v[l]).astype(BF)
            new_sums, new_dens = [], []
            for g in range(groups):
                keys = keyval[:, g * wide : (g + 1) * wide]
                values = keyval[:, width + g * wide : width + (g + 1) * wide]
                scores = lax.dot_general(
                    stacked[g], keys, (((1,), (1,)), ((), ())), preferred_element_type=F32
                )
                expo = jnp.exp2(jnp.tanh(scores * inner) * outer)
                part = dot(expo.astype(BF), values)
                total = sums[g]
                for i in range(per):
                    total = total + jnp.where(masks[i], part[i * mine : (i + 1) * mine], 0.0)
                new_sums.append(total)
                den = dens[g]
                for c in range(0, cores * mine, 128):
                    den = den + expo[:, c : c + 128]
                new_dens.append(den)
            return tuple(new_sums), tuple(new_dens)

        carry = (
            tuple(jnp.zeros((mine, wide), F32) for _ in range(groups)),
            tuple(jnp.zeros((per * mine, 128), F32) for _ in range(groups)),
        )
        for e in range(1, cores):
            other = gath.at[l, j, (me_s + cores - e) % cores]
            remote(
                other, other, nsend.at[l, e - 1], nrecv.at[l, e - 1], me_p, (me_s + e) % cores
            ).wait_recv()
        carry = round_of(j, carry)
        for d in range(1, teams):
            team = (j + teams - d) % teams
            block = gath.at[l, team, me_s]
            remote(
                block, block, gsend.at[l, d - 1], grecv.at[l, d - 1], spot * teams + team, me_s
            ).wait_recv()
            for e in range(1, cores):
                copy = remote(
                    block, block, fsend.at[l, d - 1, e - 1], frecv.at[l, d - 1, e - 1],
                    me_p, (me_s + e) % cores,
                )
                copy.start()
                sends.append(copy)
        for d in range(1, teams):
            team = (j + teams - d) % teams
            for e in range(1, cores):
                block = gath.at[l, team, (me_s + cores - e) % cores]
                remote(
                    block, block, fsend.at[l, d - 1, e - 1], frecv.at[l, d - 1, e - 1],
                    me_p, (me_s + e) % cores,
                ).wait_recv()
        if teams <= 2:
            for d in range(1, teams):
                carry = round_of((j + teams - d) % teams, carry)
        else:
            carry = lax.fori_loop(1, teams, lambda d, c: round_of((j + teams - d) % teams, c), carry)
        sums, dens = carry
        pieces = []
        for g in range(groups):
            inverse = 1.0 / jnp.sum(dens[g], axis=-1, keepdims=True)
            scale = jnp.zeros((mine, wide), F32)
            for i in range(per):
                scale = jnp.where(masks[i], inverse[i * mine : (i + 1) * mine], scale)
            pieces.append((sums[g] * scale).astype(BF))
        attended = jnp.concatenate(pieces, axis=1)
        loads["wo", l].wait()
        hidden = hidden + dot(attended, wo_v[l])
        mixed = rms_norm(hidden, gains_ref[l, 1:2, :]).astype(BF)
        loads["wu", l].wait()
        upward = jax.nn.gelu(dot(mixed, wu_v[l])).astype(BF)
        loads["wd", l].wait()
        hidden = hidden + dot(upward, wd_v[l])

    loads["fgain"].wait()
    final_rows = rms_norm(hidden, fgain_ref[...].reshape(1, width)).astype(BF)
    loads["wout"].wait()
    predicted = dot(final_rows, wout_v[...]).astype(BF)

    returns = []
    for b in range(h):
        pout[b] = predicted[b * rows : (b + 1) * rows]
        to_p, to_s, slot = (me_s * h + b) * teams + j, spot // h, spot % h
        own = (to_p == me_p) & (to_s == me_s)
        copy = remote(pout.at[b], pin.at[slot], rsend.at[b], rrecv.at[slot], to_p, to_s)
        returns.append((own, copy))

        @pl.when(jnp.logical_not(own))
        def _():
            copy.start()

        @pl.when(own)
        def _():
            pin[slot] = pout[b]

    @pl.when(me_s > 0)
    def _():
        remote(prev_v, prev_v, vsend.at[0], vrecv.at[0], me_p, (me_s + 1) % cores).wait_recv()

    @pl.when(me_s == 0)
    def _():
        prev_v[...] = start_v[...]

    loads["noise"].wait()
    loads["rates"].wait()
    loads["scales"].wait()
    first = start_v[...].reshape(rows, width)
    bases = []
    total = jnp.zeros((rows, width), F32)
    for t in range(h):
        points = (prev_v[...] if t == 0 else chain_v[t - 1]).reshape(rows, width)
        noise = noise_v[t].astype(F32).reshape(rows, width)
        total = total + (scales_ref[t] * noise - rates_ref[t] * points)
        bases.append(total)
    running = jnp.zeros((rows, width), F32)
    sums = []
    for t in range(h):
        own = ((me_s * h + t) * teams + j == me_p) & (spot // h == me_s)

        @pl.when(jnp.logical_not(own))
        def _():
            remote(
                pin.at[t], pin.at[t], rsend.at[0], rrecv.at[t], me_p, (me_s + 1) % cores
            ).wait_recv()

        running = running + rates_ref[t] * pin[t].astype(F32)
        sums.append(bases[t] + running)
    tot_out[...] = sums[-1]
    ups = []
    for d in range(1, cores):
        up = remote(tot_out, tot_in.at[d - 1], usend.at[d - 1], urecv.at[d - 1], me_p, (me_s + d) % cores)
        ups.append(up)

        @pl.when(me_s + d < cores)
        def _():
            up.start()

    for d in range(1, cores):

        @pl.when(me_s - d >= 0)
        def _():
            remote(
                tot_in.at[d - 1], tot_in.at[d - 1], usend.at[d - 1], urecv.at[d - 1],
                me_p, (me_s + cores - d) % cores,
            ).wait_recv()

    before = first
    for d in range(1, cores):
        before = before + jnp.where(me_s - d >= 0, tot_in[d - 1], 0.0)
    for t in range(h):
        out_ref[t] = (before + sums[t]).reshape(out_ref.shape[1:])

    for own, copy in scatter + returns:

        @pl.when(jnp.logical_not(own))
        def _():
            copy.wait_send()

    @pl.when(me_s < cores - 1)
    def _():
        hand.wait_send()

    for copy in shares + sends:
        copy.wait_send()
    for d, up in enumerate(ups):

        @pl.when(me_s + d + 1 < cores)
        def _():
            up.wait_send()


def local(n, cores, chain, start, noise, timesteps, rates, noise_scales, time_weight, w_query, w_keyval,
          w_attn_out, w_up, w_down, gains, final_gain, w_output):
    h, persons, tokens, width = chain.shape
    rows = persons * tokens
    layers = w_query.shape[0]
    teams = n // (h * cores)
    mine = h * rows
    sizes = (n, cores, h, rows, width, layers)
    hbm = pl.BlockSpec(memory_space=pltpu.HBM)
    vmem = pl.BlockSpec(memory_space=pltpu.VMEM)
    dma = pltpu.SemaphoreType.DMA
    peers, teamed = max(cores - 1, 1), max(teams - 1, 1)
    scratch = [
        pltpu.SMEM(timesteps.shape, jnp.int32), pltpu.SMEM(rates.shape, F32), pltpu.SMEM(rates.shape, F32),
        pltpu.VMEM(gains.shape, F32), pltpu.VMEM(final_gain.shape, F32),
        pltpu.VMEM(chain.shape, F32), pltpu.VMEM(start.shape, F32), pltpu.VMEM(noise.shape, BF),
        pltpu.VMEM(time_weight.shape, BF), pltpu.VMEM(w_query.shape, BF), pltpu.VMEM(w_keyval.shape, BF),
        pltpu.VMEM(w_attn_out.shape, BF), pltpu.VMEM(w_up.shape, BF), pltpu.VMEM(w_down.shape, BF),
        pltpu.VMEM(w_output.shape, BF),
        pltpu.VMEM((h, rows, width), BF), pltpu.VMEM((h, rows, width), BF),
        pltpu.VMEM((cores, 8, width), F32), pltpu.VMEM(start.shape, F32),
        pltpu.VMEM((layers, teams, cores, mine, width), BF),
        pltpu.VMEM((h, rows, width), BF), pltpu.VMEM((h, rows, width), BF),
        pltpu.VMEM((rows, width), F32), pltpu.VMEM((peers, rows, width), F32),
        dma((10 + 5 * layers,)), dma((h,)), dma((h,)), dma((peers,)), dma((peers,)), dma((1,)), dma((1,)),
        dma((layers, teamed)), dma((layers, teamed)), dma((layers, peers)), dma((layers, peers)),
        dma((layers, teamed, peers)), dma((layers, teamed, peers)),
        dma((h,)), dma((h,)), dma((peers,)), dma((peers,)),
    ]
    return pl.pallas_call(
        functools.partial(kernel, sizes),
        out_shape=jax.ShapeDtypeStruct(chain.shape, F32),
        in_specs=[hbm] * 15,
        out_specs=vmem,
        scratch_shapes=scratch,
        compiler_params=pltpu.CompilerParams(
            collective_id=0, has_side_effects=True, vmem_limit_bytes=60 * 1024 * 1024
        ),
    )(
        chain, start, noise, timesteps, rates, noise_scales, time_weight, w_query, w_keyval, w_attn_out,
        w_up, w_down, gains, final_gain, w_output,
    )


def solution(mesh):
    placed = (
        P(("groups", "step"), "person", None, None),
        P(("groups", "person"), None, None),
        P(("groups", "step"), "person", None, None),
        P(("groups", "step")),
        P(("groups", "step")),
        P(("groups", "step")),
    ) + (P(),) * 9
    return jax.shard_map(
        functools.partial(local, mesh.shape["person"], mesh.shape["step"]),
        mesh=mesh,
        in_specs=placed,
        out_specs=P(("groups", "step"), "person", None, None),
        check_vma=False,
    )
```

```python
import functools
import math

import jax
import jax.numpy as jnp
from jax import lax
from jax.experimental import pallas as pl
from jax.experimental.pallas import tpu as pltpu
from jax.sharding import PartitionSpec as P

HEADS = 8
MESH = pl.DeviceIdType.MESH
BF = jnp.bfloat16
F32 = jnp.float32


def dot(a, b):
    return jnp.dot(a, b, preferred_element_type=F32)


def rms_norm(values, gain):
    return values * lax.rsqrt(jnp.mean(values * values, axis=-1, keepdims=True) + 1e-06) * gain


def kernel(
    sizes,
    chain_ref, start_ref, noise_ref, times_hbm, rates_hbm, scales_hbm,
    tw_ref, wq_ref, wkv_ref, wo_ref, wu_ref, wd_ref, gains_hbm, fgain_hbm, wout_ref,
    out_ref,
    times_ref, rates_ref, scales_ref, gains_ref, fgain_ref, chain_v, start_v, noise_v, tw_v, wq_v, wkv_v, wo_v, wu_v, wd_v, wout_v,
    send_v, rows_v, temb_v, prev_v, gath, hid_v, stack_v, keyval_v, sum_v, den_v, att_v, pout, pin, tot_out, tot_in,
    load_sem, ssend, srecv, tsend, trecv, vsend, vrecv, ysend, yrecv, nsend, nrecv,
    rsend, rrecv, usend, urecv,
):
    n, cores, h, rows, width, layers = sizes
    window = h * cores
    teams = n // window
    mine = h * rows
    me_p, me_s = lax.axis_index("person"), lax.axis_index("step")
    spot, j = me_p // teams, me_p % teams

    def device(person, step):
        return {"person": person, "step": step}

    def remote(src, dst, send_sem, recv_sem, person, step):
        return pltpu.make_async_remote_copy(
            src_ref=src, dst_ref=dst, send_sem=send_sem, recv_sem=recv_sem,
            device_id=device(person, step), device_id_type=MESH,
        )

    loads = {}

    def load(name, src, dst):
        copy = pltpu.make_async_copy(src, dst, load_sem.at[len(loads)])
        loads[name] = copy
        copy.start()

    load("chain", chain_ref, chain_v)
    load("start", start_ref, start_v)
    load("times", times_hbm, times_ref)
    load("tw", tw_ref, tw_v)
    load("gains", gains_hbm, gains_ref)
    for l in range(layers):
        load(("wq", l), wq_ref.at[l], wq_v.at[l])
        load(("wkv", l), wkv_ref.at[l], wkv_v.at[l])
        load(("wo", l), wo_ref.at[l], wo_v.at[l])
        load(("wu", l), wu_ref.at[l], wu_v.at[l])
        load(("wd", l), wd_ref.at[l], wd_v.at[l])
    load("wout", wout_ref, wout_v)
    load("noise", noise_ref, noise_v)
    load("fgain", fgain_hbm, fgain_ref)
    load("rates", rates_hbm, rates_ref)
    load("scales", scales_hbm, scales_ref)

    barrier = pltpu.get_barrier_semaphore()
    for dq in range(window):
        for ds in range(cores):
            if dq or ds:
                pl.semaphore_signal(
                    barrier, inc=1,
                    device_id=device(((spot + dq) % window) * teams + j, (me_s + ds) % cores),
                    device_id_type=MESH,
                )
    for d in range(1, teams):
        pl.semaphore_signal(
            barrier, inc=1, device_id=device(spot * teams + (j + d) % teams, me_s), device_id_type=MESH
        )

    loads["chain"].wait()
    loads["start"].wait()
    is_last = me_s == cores - 1
    for t in range(h):
        block = chain_v[t].reshape(rows, width)
        if t == h - 1:
            block = jnp.where(is_last, start_v[...].reshape(rows, width), block)
        send_v[t] = block.astype(BF)
    pl.semaphore_wait(barrier, window * cores - 1 + teams - 1)

    scatter = []
    for t in range(h):
        position = (me_s * h + t + 1) % window
        to_p, to_s, slot = position * teams + j, spot // h, spot % h
        own = (to_p == me_p) & (to_s == me_s)
        copy = remote(send_v.at[t], rows_v.at[0, slot], ssend.at[t], srecv.at[slot], to_p, to_s)
        scatter.append((own, copy))

        @pl.when(jnp.logical_not(own))
        def _():
            copy.start()

        @pl.when(own)
        def _():
            rows_v[0, slot] = send_v[t]

    hand = remote(chain_v.at[h - 1], prev_v, vsend.at[0], vrecv.at[0], me_p, (me_s + 1) % cores)

    @pl.when(me_s < cores - 1)
    def _():
        hand.start()

    lane = lax.broadcasted_iota(jnp.int32, (8, width), 1)
    sub = lax.broadcasted_iota(jnp.int32, (8, width), 0)
    half = width // 2
    index = jnp.where(lane < half, lane, lane - half).astype(F32)
    freqs = jnp.exp(-math.log(10000.0) * index / half)
    when = jnp.zeros((8, width), F32)
    loads["times"].wait()
    for t in range(h):
        when = jnp.where(sub == t, times_ref[t].astype(F32), when)
    angles = when * freqs
    features = jnp.where(lane < half, jnp.sin(angles), jnp.cos(angles)).astype(BF)
    loads["tw"].wait()
    temb = dot(features, tw_v[...])
    temb_v[me_s] = temb * (1.0 / (1.0 + jnp.exp(-temb)))
    shares = []
    for d in range(1, cores):
        share = remote(
            temb_v.at[me_s], temb_v.at[me_s], tsend.at[d - 1], trecv.at[d - 1], me_p, (me_s + d) % cores
        )
        share.start()
        shares.append(share)
    sends = []
    from_s = ((spot + window - 1) % window) // h
    for b in range(h):
        own = (me_s * h + b == spot) & (from_s == me_s)

        @pl.when(jnp.logical_not(own))
        def _():
            remote(
                rows_v.at[0, b], rows_v.at[0, b], ssend.at[0], srecv.at[b], me_p, (me_s + 1) % cores
            ).wait_recv()

        for d in range(1, teams):
            copy = remote(
                rows_v.at[0, b], rows_v.at[d, b], ysend.at[d - 1, b], yrecv.at[d - 1, b],
                spot * teams + (j + d) % teams, me_s,
            )
            copy.start()
            sends.append(copy)

    for d in range(1, cores):
        other = (me_s + cores - d) % cores
        remote(temb_v.at[other], temb_v.at[other], tsend.at[d - 1], trecv.at[d - 1], me_p, other).wait_recv()
    time_row = temb_v[spot // h, pl.ds(spot % h, 1), :]

    head_dim = width // HEADS
    wide = min(256, width)
    per = wide // head_dim
    groups = width // wide
    masks = [lax.broadcasted_iota(jnp.int32, (mine, wide), 1) // head_dim == i for i in range(per)]
    inner = 1.0 / (math.sqrt(head_dim) * 30.0)
    outer = 30.0 * math.log2(math.e)

    def each(low, high, act):
        if high - low <= 2:
            for r in range(low, high):
                act(r)
        else:

            @pl.loop(low, high)
            def _(r):
                act(r)

    def share(l, r, e):
        return remote(
            gath.at[l, 0, r], gath.at[l, e, r], nsend.at[l, e - 1, r], nrecv.at[l, e - 1, r],
            me_p, (me_s + e) % cores,
        )

    def arrive(r):
        for b in range(h):
            remote(
                rows_v.at[r, b], rows_v.at[r, b], ysend.at[r - 1, b], yrecv.at[r - 1, b],
                me_p, (me_s + 1) % cores,
            ).wait_recv()

    def begin(r):
        hid_v[r] = rows_v[r].reshape(mine, width).astype(F32) + time_row

    def normalize(l, r):
        gath[l, 0, r] = rms_norm(hid_v[r], gains_ref[l, 0:1, :]).astype(BF)
        for e in range(1, cores):
            share(l, r, e).start()

    def query(l, r):
        queries = dot(gath[l, 0, r], wq_v[l]).astype(BF)
        for g in range(groups):
            piece = queries[:, g * wide : (g + 1) * wide]
            for i in range(per):
                stack_v[r, g, i * mine : (i + 1) * mine, :] = jnp.where(masks[i], piece, jnp.zeros_like(piece))

    def keys_of(l, r):
        for e in range(1, cores):
            share(l, r, e).wait_recv()
        keyval_v[r] = dot(gath[l, :, r].reshape(cores * mine, width), wkv_v[l]).astype(BF)

    def attend(r, k, fresh):
        for g in range(groups):
            keys = keyval_v[k, :, g * wide : (g + 1) * wide]
            values = keyval_v[k, :, width + g * wide : width + (g + 1) * wide]
            scores = lax.dot_general(
                stack_v[r, g], keys, (((1,), (1,)), ((), ())), preferred_element_type=F32
            )
            expo = jnp.exp2(jnp.tanh(scores * inner) * outer)
            part = dot(expo.astype(BF), values)
            total = part[:mine]
            for i in range(1, per):
                total = jnp.where(masks[i], part[i * mine : (i + 1) * mine], total)
            den = expo[:, :128]
            for c in range(128, cores * mine, 128):
                den = den + expo[:, c : c + 128]
            if fresh:
                sum_v[r, g] = total
                den_v[r, g] = den
            else:
                sum_v[r, g] = sum_v[r, g] + total
                den_v[r, g] = den_v[r, g] + den

    def finish(r):
        for g in range(groups):
            inverse = 1.0 / jnp.sum(den_v[r, g], axis=-1, keepdims=True)
            scale = jnp.broadcast_to(inverse[:mine], (mine, wide))
            for i in range(1, per):
                scale = jnp.where(masks[i], inverse[i * mine : (i + 1) * mine], scale)
            att_v[r, :, g * wide : (g + 1) * wide] = (sum_v[r, g] * scale).astype(BF)

    def feed(l, r, count):
        part = pl.ds(r, count)
        hidden = hid_v[part].reshape(count * mine, width)
        hidden = hidden + dot(att_v[part].reshape(count * mine, width), wo_v[l])
        mixed = rms_norm(hidden, gains_ref[l, 1:2, :]).astype(BF)
        upward = jax.nn.gelu(dot(mixed, wu_v[l])).astype(BF)
        hidden = hidden + dot(upward, wd_v[l])
        hid_v[part] = hidden.reshape(count, mine, width)

    loads["gains"].wait()
    for l in range(layers):
        active = teams if l < layers - 1 else 1
        if l == 0:
            begin(0)
            normalize(l, 0)
        else:
            each(0, teams, lambda r: normalize(l, r))
        loads["wq", l].wait()
        query(l, 0)
        loads["wkv", l].wait()
        keys_of(l, 0)
        attend(0, 0, True)
        if l == 0:

            def enter(r):
                arrive(r)
                begin(r)
                normalize(l, r)

            each(1, teams, enter)

        def follow(r):
            query(l, r)
            attend(r, 0, True)

        each(1, active, follow)

        def sweep(k):
            keys_of(l, k)
            each(0, active, lambda r: attend(r, k, False))

        each(1, teams, sweep)
        each(0, active, finish)
        loads["wo", l].wait()
        loads["wu", l].wait()
        loads["wd", l].wait()
        if active <= 2:
            feed(l, 0, active)
        else:
            each(0, active, lambda r: feed(l, r, 1))

    hidden = hid_v[0]
    loads["fgain"].wait()
    final_rows = rms_norm(hidden, fgain_ref[...].reshape(1, width)).astype(BF)
    loads["wout"].wait()
    predicted = dot(final_rows, wout_v[...]).astype(BF)

    returns = []
    for b in range(h):
        pout[b] = predicted[b * rows : (b + 1) * rows]
        to_p, to_s, slot = (me_s * h + b) * teams + j, spot // h, spot % h
        own = (to_p == me_p) & (to_s == me_s)
        copy = remote(pout.at[b], pin.at[slot], rsend.at[b], rrecv.at[slot], to_p, to_s)
        returns.append((own, copy))

        @pl.when(jnp.logical_not(own))
        def _():
            copy.start()

        @pl.when(own)
        def _():
            pin[slot] = pout[b]

    @pl.when(me_s > 0)
    def _():
        remote(prev_v, prev_v, vsend.at[0], vrecv.at[0], me_p, (me_s + 1) % cores).wait_recv()

    @pl.when(me_s == 0)
    def _():
        prev_v[...] = start_v[...]

    loads["noise"].wait()
    loads["rates"].wait()
    loads["scales"].wait()
    first = start_v[...].reshape(rows, width)
    bases = []
    total = jnp.zeros((rows, width), F32)
    for t in range(h):
        points = (prev_v[...] if t == 0 else chain_v[t - 1]).reshape(rows, width)
        noise = noise_v[t].astype(F32).reshape(rows, width)
        total = total + (scales_ref[t] * noise - rates_ref[t] * points)
        bases.append(total)
    running = jnp.zeros((rows, width), F32)
    sums = []
    for t in range(h):
        own = ((me_s * h + t) * teams + j == me_p) & (spot // h == me_s)

        @pl.when(jnp.logical_not(own))
        def _():
            remote(
                pin.at[t], pin.at[t], rsend.at[0], rrecv.at[t], me_p, (me_s + 1) % cores
            ).wait_recv()

        running = running + rates_ref[t] * pin[t].astype(F32)
        sums.append(bases[t] + running)
    tot_out[...] = sums[-1]
    ups = []
    for d in range(1, cores):
        up = remote(tot_out, tot_in.at[d - 1], usend.at[d - 1], urecv.at[d - 1], me_p, (me_s + d) % cores)
        ups.append(up)

        @pl.when(me_s + d < cores)
        def _():
            up.start()

    for d in range(1, cores):

        @pl.when(me_s - d >= 0)
        def _():
            remote(
                tot_in.at[d - 1], tot_in.at[d - 1], usend.at[d - 1], urecv.at[d - 1],
                me_p, (me_s + cores - d) % cores,
            ).wait_recv()

    before = first
    for d in range(1, cores):
        before = before + jnp.where(me_s - d >= 0, tot_in[d - 1], 0.0)
    for t in range(h):
        out_ref[t] = (before + sums[t]).reshape(out_ref.shape[1:])

    for own, copy in scatter + returns:

        @pl.when(jnp.logical_not(own))
        def _():
            copy.wait_send()

    @pl.when(me_s < cores - 1)
    def _():
        hand.wait_send()

    for copy in shares + sends:
        copy.wait_send()
    for l in range(layers):
        for e in range(1, cores):
            each(0, teams, lambda r: share(l, r, e).wait_send())
    for d, up in enumerate(ups):

        @pl.when(me_s + d + 1 < cores)
        def _():
            up.wait_send()


def local(n, cores, chain, start, noise, timesteps, rates, noise_scales, time_weight, w_query, w_keyval,
          w_attn_out, w_up, w_down, gains, final_gain, w_output):
    h, persons, tokens, width = chain.shape
    rows = persons * tokens
    layers = w_query.shape[0]
    teams = n // (h * cores)
    mine = h * rows
    sizes = (n, cores, h, rows, width, layers)
    hbm = pl.BlockSpec(memory_space=pltpu.HBM)
    vmem = pl.BlockSpec(memory_space=pltpu.VMEM)
    dma = pltpu.SemaphoreType.DMA
    wide = min(256, width)
    per, groups = wide * HEADS // width, width // wide
    peers, teamed = max(cores - 1, 1), max(teams - 1, 1)
    scratch = [
        pltpu.SMEM(timesteps.shape, jnp.int32), pltpu.SMEM(rates.shape, F32), pltpu.SMEM(rates.shape, F32),
        pltpu.VMEM(gains.shape, F32), pltpu.VMEM(final_gain.shape, F32),
        pltpu.VMEM(chain.shape, F32), pltpu.VMEM(start.shape, F32), pltpu.VMEM(noise.shape, BF),
        pltpu.VMEM(time_weight.shape, BF), pltpu.VMEM(w_query.shape, BF), pltpu.VMEM(w_keyval.shape, BF),
        pltpu.VMEM(w_attn_out.shape, BF), pltpu.VMEM(w_up.shape, BF), pltpu.VMEM(w_down.shape, BF),
        pltpu.VMEM(w_output.shape, BF),
        pltpu.VMEM((h, rows, width), BF), pltpu.VMEM((teams, h, rows, width), BF),
        pltpu.VMEM((cores, 8, width), F32), pltpu.VMEM(start.shape, F32),
        pltpu.VMEM((layers, cores, teams, mine, width), BF), pltpu.VMEM((teams, mine, width), F32),
        pltpu.VMEM((teams, groups, per * mine, wide), BF), pltpu.VMEM((teams, cores * mine, 2 * width), BF),
        pltpu.VMEM((teams, groups, mine, wide), F32), pltpu.VMEM((teams, groups, per * mine, 128), F32),
        pltpu.VMEM((teams, mine, width), BF),
        pltpu.VMEM((h, rows, width), BF), pltpu.VMEM((h, rows, width), BF),
        pltpu.VMEM((rows, width), F32), pltpu.VMEM((peers, rows, width), F32),
        dma((10 + 5 * layers,)), dma((h,)), dma((h,)), dma((peers,)), dma((peers,)), dma((1,)), dma((1,)),
        dma((teamed, h)), dma((teamed, h)), dma((layers, peers, teams)), dma((layers, peers, teams)),
        dma((h,)), dma((h,)), dma((peers,)), dma((peers,)),
    ]
    return pl.pallas_call(
        functools.partial(kernel, sizes),
        out_shape=jax.ShapeDtypeStruct(chain.shape, F32),
        in_specs=[hbm] * 15,
        out_specs=vmem,
        scratch_shapes=scratch,
        compiler_params=pltpu.CompilerParams(
            collective_id=0, has_side_effects=True, vmem_limit_bytes=60 * 1024 * 1024
        ),
    )(
        chain, start, noise, timesteps, rates, noise_scales, time_weight, w_query, w_keyval, w_attn_out,
        w_up, w_down, gains, final_gain, w_output,
    )


def solution(mesh):
    placed = (
        P(("groups", "step"), "person", None, None),
        P(("groups", "person"), None, None),
        P(("groups", "step"), "person", None, None),
        P(("groups", "step")),
        P(("groups", "step")),
        P(("groups", "step")),
    ) + (P(),) * 9
    return jax.shard_map(
        functools.partial(local, mesh.shape["person"], mesh.shape["step"]),
        mesh=mesh,
        in_specs=placed,
        out_specs=P(("groups", "step"), "person", None, None),
        check_vma=False,
    )
```

```python
import functools
import math

import jax
import jax.numpy as jnp
from jax import lax
from jax.experimental import pallas as pl
from jax.experimental.pallas import tpu as pltpu
from jax.sharding import PartitionSpec as P

HEADS = 8
MESH = pl.DeviceIdType.MESH
BF = jnp.bfloat16
F32 = jnp.float32


def dot(a, b):
    return jnp.dot(a, b, preferred_element_type=F32)


def rms_norm(values, gain):
    return values * lax.rsqrt(jnp.mean(values * values, axis=-1, keepdims=True) + 1e-06) * gain


def kernel(
    sizes,
    chain_ref, start_ref, noise_ref, times_hbm, rates_hbm, scales_hbm,
    tw_ref, wq_ref, wkv_ref, wo_ref, wu_ref, wd_ref, gains_hbm, fgain_hbm, wout_ref,
    out_ref,
    times_ref, rates_ref, scales_ref, gains_ref, fgain_ref, chain_v, start_v, noise_v, tw_v, wq_v, wkv_v, wo_v, wu_v, wd_v, wout_v,
    send_v, rows_v, temb_v, prev_v, gath, hid_v, stack_v, keyval_v, sum_v, den_v, att_v, pout, pin, tot_out, tot_in,
    load_sem, ssend, srecv, tsend, trecv, vsend, vrecv, ysend, yrecv, nsend, nrecv,
    rsend, rrecv, usend, urecv,
):
    n, cores, h, rows, width, layers = sizes
    window = h * cores
    teams = n // window
    mine = h * rows
    me_p, me_s = lax.axis_index("person"), lax.axis_index("step")
    spot, j = me_p // teams, me_p % teams

    def device(person, step):
        return {"person": person, "step": step}

    def remote(src, dst, send_sem, recv_sem, person, step):
        return pltpu.make_async_remote_copy(
            src_ref=src, dst_ref=dst, send_sem=send_sem, recv_sem=recv_sem,
            device_id=device(person, step), device_id_type=MESH,
        )

    loads = {}

    def load(name, src, dst):
        copy = pltpu.make_async_copy(src, dst, load_sem.at[len(loads)])
        loads[name] = copy
        copy.start()

    load("chain", chain_ref, chain_v)
    load("start", start_ref, start_v)
    load("times", times_hbm, times_ref)
    load("tw", tw_ref, tw_v)
    load("gains", gains_hbm, gains_ref)
    for l in range(layers):
        load(("wq", l), wq_ref.at[l], wq_v.at[l])
        load(("wkv", l), wkv_ref.at[l], wkv_v.at[l])
        load(("wo", l), wo_ref.at[l], wo_v.at[l])
        load(("wu", l), wu_ref.at[l], wu_v.at[l])
        load(("wd", l), wd_ref.at[l], wd_v.at[l])
    load("wout", wout_ref, wout_v)
    load("noise", noise_ref, noise_v)
    load("fgain", fgain_hbm, fgain_ref)
    load("rates", rates_hbm, rates_ref)
    load("scales", scales_hbm, scales_ref)

    barrier = pltpu.get_barrier_semaphore()
    for dq in range(window):
        for ds in range(cores):
            if dq or ds:
                pl.semaphore_signal(
                    barrier, inc=1,
                    device_id=device(((spot + dq) % window) * teams + j, (me_s + ds) % cores),
                    device_id_type=MESH,
                )
    for d in range(1, teams):
        pl.semaphore_signal(
            barrier, inc=1, device_id=device(spot * teams + (j + d) % teams, me_s), device_id_type=MESH
        )

    loads["chain"].wait()
    loads["start"].wait()
    is_last = me_s == cores - 1
    for t in range(h):
        block = chain_v[t].reshape(rows, width)
        if t == h - 1:
            block = jnp.where(is_last, start_v[...].reshape(rows, width), block)
        send_v[t] = block.astype(BF)
    pl.semaphore_wait(barrier, window * cores - 1 + teams - 1)

    scatter = []
    for t in range(h):
        position = (me_s * h + t + 1) % window
        to_p, to_s, slot = position * teams + j, spot // h, spot % h
        own = (to_p == me_p) & (to_s == me_s)
        copy = remote(send_v.at[t], rows_v.at[0, slot], ssend.at[t], srecv.at[slot], to_p, to_s)
        scatter.append((own, copy))

        @pl.when(jnp.logical_not(own))
        def _():
            copy.start()

        @pl.when(own)
        def _():
            rows_v[0, slot] = send_v[t]

    hand = remote(chain_v.at[h - 1], prev_v, vsend.at[0], vrecv.at[0], me_p, (me_s + 1) % cores)

    @pl.when(me_s < cores - 1)
    def _():
        hand.start()

    lane = lax.broadcasted_iota(jnp.int32, (8, width), 1)
    sub = lax.broadcasted_iota(jnp.int32, (8, width), 0)
    half = width // 2
    index = jnp.where(lane < half, lane, lane - half).astype(F32)
    freqs = jnp.exp(-math.log(10000.0) * index / half)
    when = jnp.zeros((8, width), F32)
    loads["times"].wait()
    for t in range(h):
        when = jnp.where(sub == t, times_ref[t].astype(F32), when)
    angles = when * freqs
    features = jnp.where(lane < half, jnp.sin(angles), jnp.cos(angles)).astype(BF)
    loads["tw"].wait()
    temb = dot(features, tw_v[...])
    temb_v[me_s] = temb * (1.0 / (1.0 + jnp.exp(-temb)))
    shares = []
    for d in range(1, cores):
        share = remote(
            temb_v.at[me_s], temb_v.at[me_s], tsend.at[d - 1], trecv.at[d - 1], me_p, (me_s + d) % cores
        )
        share.start()
        shares.append(share)
    sends = []
    from_s = ((spot + window - 1) % window) // h
    for b in range(h):
        own = (me_s * h + b == spot) & (from_s == me_s)

        @pl.when(jnp.logical_not(own))
        def _():
            remote(
                rows_v.at[0, b], rows_v.at[0, b], ssend.at[0], srecv.at[b], me_p, (me_s + 1) % cores
            ).wait_recv()

        for d in range(1, teams):
            copy = remote(
                rows_v.at[0, b], rows_v.at[d, b], ysend.at[d - 1, b], yrecv.at[d - 1, b],
                spot * teams + (j + d) % teams, me_s,
            )
            copy.start()
            sends.append(copy)

    for d in range(1, cores):
        other = (me_s + cores - d) % cores
        remote(temb_v.at[other], temb_v.at[other], tsend.at[d - 1], trecv.at[d - 1], me_p, other).wait_recv()
    time_row = temb_v[spot // h, pl.ds(spot % h, 1), :]

    head_dim = width // HEADS
    wide = min(256, width)
    per = wide // head_dim
    groups = width // wide
    masks = [lax.broadcasted_iota(jnp.int32, (mine, wide), 1) // head_dim == i for i in range(per)]
    inner = 1.0 / (math.sqrt(head_dim) * 30.0)
    outer = 30.0 * math.log2(math.e)

    def each(low, high, act):
        if high - low <= 2:
            for r in range(low, high):
                act(r)
        else:

            @pl.loop(low, high)
            def _(r):
                act(r)

    def share(l, r, e):
        return remote(
            gath.at[l, 0, r], gath.at[l, e, r], nsend.at[l, e - 1, r], nrecv.at[l, e - 1, r],
            me_p, (me_s + e) % cores,
        )

    def arrive(r):
        for b in range(h):
            remote(
                rows_v.at[r, b], rows_v.at[r, b], ysend.at[r - 1, b], yrecv.at[r - 1, b],
                me_p, (me_s + 1) % cores,
            ).wait_recv()

    def begin(r):
        hid_v[r] = rows_v[r].reshape(mine, width).astype(F32) + time_row

    def normalize(l, r):
        gath[l, 0, r] = rms_norm(hid_v[r], gains_ref[l, 0:1, :]).astype(BF)
        for e in range(1, cores):
            share(l, r, e).start()

    def query(l, r):
        queries = dot(gath[l, 0, r], wq_v[l]).astype(BF)
        for g in range(groups):
            piece = queries[:, g * wide : (g + 1) * wide]
            for i in range(per):
                stack_v[r, g, i * mine : (i + 1) * mine, :] = jnp.where(masks[i], piece, jnp.zeros_like(piece))

    def keys_of(l, r):
        for e in range(1, cores):
            share(l, r, e).wait_recv()
        keyval_v[r] = dot(gath[l, :, r].reshape(cores * mine, width), wkv_v[l]).astype(BF)

    def attend(r, k, fresh):
        for g in range(groups):
            keys = keyval_v[k, :, g * wide : (g + 1) * wide]
            values = keyval_v[k, :, width + g * wide : width + (g + 1) * wide]
            scores = lax.dot_general(
                stack_v[r, g], keys, (((1,), (1,)), ((), ())), preferred_element_type=F32
            )
            expo = jnp.exp2(jnp.tanh(scores * inner) * outer)
            part = dot(expo.astype(BF), values)
            total = part[:mine]
            for i in range(1, per):
                total = jnp.where(masks[i], part[i * mine : (i + 1) * mine], total)
            den = expo[:, :128]
            for c in range(128, cores * mine, 128):
                den = den + expo[:, c : c + 128]
            if fresh:
                sum_v[r, g] = total
                den_v[r, g] = den
            else:
                sum_v[r, g] = sum_v[r, g] + total
                den_v[r, g] = den_v[r, g] + den

    def finish(r):
        for g in range(groups):
            inverse = 1.0 / jnp.sum(den_v[r, g], axis=-1, keepdims=True)
            scale = jnp.broadcast_to(inverse[:mine], (mine, wide))
            for i in range(1, per):
                scale = jnp.where(masks[i], inverse[i * mine : (i + 1) * mine], scale)
            att_v[r, :, g * wide : (g + 1) * wide] = (sum_v[r, g] * scale).astype(BF)

    def feed(l, r, count):
        part = pl.ds(r, count)
        hidden = hid_v[part].reshape(count * mine, width)
        hidden = hidden + dot(att_v[part].reshape(count * mine, width), wo_v[l])
        mixed = rms_norm(hidden, gains_ref[l, 1:2, :]).astype(BF)
        upward = jax.nn.gelu(dot(mixed, wu_v[l])).astype(BF)
        hidden = hidden + dot(upward, wd_v[l])
        hid_v[part] = hidden.reshape(count, mine, width)

    loads["gains"].wait()
    for l in range(layers):
        active = teams if l < layers - 1 else 1
        if l == 0:
            begin(0)
            normalize(l, 0)
        else:
            each(0, teams, lambda r: normalize(l, r))
        loads["wq", l].wait()
        query(l, 0)
        loads["wkv", l].wait()
        keys_of(l, 0)
        attend(0, 0, True)
        if l == 0:

            def enter(r):
                arrive(r)
                begin(r)
                normalize(l, r)

            each(1, teams, enter)

        def follow(r):
            query(l, r)
            attend(r, 0, True)

        each(1, active, follow)

        def sweep(k):
            keys_of(l, k)
            each(0, active, lambda r: attend(r, k, False))

        each(1, teams, sweep)
        each(0, active, finish)
        loads["wo", l].wait()
        loads["wu", l].wait()
        loads["wd", l].wait()
        if active <= 2:
            feed(l, 0, active)
        else:
            each(0, active, lambda r: feed(l, r, 1))

    hidden = hid_v[0]
    loads["fgain"].wait()
    final_rows = rms_norm(hidden, fgain_ref[...].reshape(1, width)).astype(BF)
    loads["wout"].wait()
    predicted = dot(final_rows, wout_v[...]).astype(BF)

    returns = []
    for b in range(h):
        pout[b] = predicted[b * rows : (b + 1) * rows]
        to_p, to_s, slot = (me_s * h + b) * teams + j, spot // h, spot % h
        own = (to_p == me_p) & (to_s == me_s)
        copy = remote(pout.at[b], pin.at[slot], rsend.at[b], rrecv.at[slot], to_p, to_s)
        returns.append((own, copy))

        @pl.when(jnp.logical_not(own))
        def _():
            copy.start()

        @pl.when(own)
        def _():
            pin[slot] = pout[b]

    @pl.when(me_s > 0)
    def _():
        remote(prev_v, prev_v, vsend.at[0], vrecv.at[0], me_p, (me_s + 1) % cores).wait_recv()

    @pl.when(me_s == 0)
    def _():
        prev_v[...] = start_v[...]

    loads["noise"].wait()
    loads["rates"].wait()
    loads["scales"].wait()
    first = start_v[...].reshape(rows, width)
    bases = []
    total = jnp.zeros((rows, width), F32)
    for t in range(h):
        points = (prev_v[...] if t == 0 else chain_v[t - 1]).reshape(rows, width)
        noise = noise_v[t].astype(F32).reshape(rows, width)
        total = total + (scales_ref[t] * noise - rates_ref[t] * points)
        bases.append(total)
    running = jnp.zeros((rows, width), F32)
    sums = []
    for t in range(h):
        own = ((me_s * h + t) * teams + j == me_p) & (spot // h == me_s)

        @pl.when(jnp.logical_not(own))
        def _():
            remote(
                pin.at[t], pin.at[t], rsend.at[0], rrecv.at[t], me_p, (me_s + 1) % cores
            ).wait_recv()

        running = running + rates_ref[t] * pin[t].astype(F32)
        sums.append(bases[t] + running)
    tot_out[...] = sums[-1]
    ups = []
    for d in range(1, cores):
        up = remote(tot_out, tot_in.at[d - 1], usend.at[d - 1], urecv.at[d - 1], me_p, (me_s + d) % cores)
        ups.append(up)

        @pl.when(me_s + d < cores)
        def _():
            up.start()

    for d in range(1, cores):

        @pl.when(me_s - d >= 0)
        def _():
            remote(
                tot_in.at[d - 1], tot_in.at[d - 1], usend.at[d - 1], urecv.at[d - 1],
                me_p, (me_s + cores - d) % cores,
            ).wait_recv()

    before = first
    for d in range(1, cores):
        before = before + jnp.where(me_s - d >= 0, tot_in[d - 1], 0.0)
    for t in range(h):
        out_ref[t] = (before + sums[t]).reshape(out_ref.shape[1:])

    for own, copy in scatter + returns:

        @pl.when(jnp.logical_not(own))
        def _():
            copy.wait_send()

    @pl.when(me_s < cores - 1)
    def _():
        hand.wait_send()

    for copy in shares + sends:
        copy.wait_send()
    for l in range(layers):
        for e in range(1, cores):
            each(0, teams, lambda r: share(l, r, e).wait_send())
    for d, up in enumerate(ups):

        @pl.when(me_s + d + 1 < cores)
        def _():
            up.wait_send()


def local(n, cores, chain, start, noise, timesteps, rates, noise_scales, time_weight, w_query, w_keyval,
          w_attn_out, w_up, w_down, gains, final_gain, w_output):
    h, persons, tokens, width = chain.shape
    rows = persons * tokens
    layers = w_query.shape[0]
    teams = n // (h * cores)
    mine = h * rows
    sizes = (n, cores, h, rows, width, layers)
    hbm = pl.BlockSpec(memory_space=pltpu.HBM)
    vmem = pl.BlockSpec(memory_space=pltpu.VMEM)
    dma = pltpu.SemaphoreType.DMA
    wide = min(256, width)
    per, groups = wide * HEADS // width, width // wide
    peers, teamed = max(cores - 1, 1), max(teams - 1, 1)
    scratch = [
        pltpu.SMEM(timesteps.shape, jnp.int32), pltpu.SMEM(rates.shape, F32), pltpu.SMEM(rates.shape, F32),
        pltpu.VMEM(gains.shape, F32), pltpu.VMEM(final_gain.shape, F32),
        pltpu.VMEM(chain.shape, F32), pltpu.VMEM(start.shape, F32), pltpu.VMEM(noise.shape, BF),
        pltpu.VMEM(time_weight.shape, BF), pltpu.VMEM(w_query.shape, BF), pltpu.VMEM(w_keyval.shape, BF),
        pltpu.VMEM(w_attn_out.shape, BF), pltpu.VMEM(w_up.shape, BF), pltpu.VMEM(w_down.shape, BF),
        pltpu.VMEM(w_output.shape, BF),
        pltpu.VMEM((h, rows, width), BF), pltpu.VMEM((teams, h, rows, width), BF),
        pltpu.VMEM((cores, 8, width), F32), pltpu.VMEM(start.shape, F32),
        pltpu.VMEM((layers, cores, teams, mine, width), BF), pltpu.VMEM((teams, mine, width), F32),
        pltpu.VMEM((teams, groups, per * mine, wide), BF), pltpu.VMEM((teams, cores * mine, 2 * width), BF),
        pltpu.VMEM((teams, groups, mine, wide), F32), pltpu.VMEM((teams, groups, per * mine, 128), F32),
        pltpu.VMEM((teams, mine, width), BF),
        pltpu.VMEM((h, rows, width), BF), pltpu.VMEM((h, rows, width), BF),
        pltpu.VMEM((rows, width), F32), pltpu.VMEM((peers, rows, width), F32),
        dma((10 + 5 * layers,)), dma((h,)), dma((h,)), dma((peers,)), dma((peers,)), dma((1,)), dma((1,)),
        dma((teamed, h)), dma((teamed, h)), dma((layers, peers, teams)), dma((layers, peers, teams)),
        dma((h,)), dma((h,)), dma((peers,)), dma((peers,)),
    ]
    chain, start, noise, timesteps, rates, noise_scales, time_weight, w_query, w_keyval, w_attn_out, w_up, w_down, gains, final_gain, w_output = (
        pltpu.with_memory_space_constraint(array, pltpu.HBM)
        for array in (
            chain, start, noise, timesteps, rates, noise_scales, time_weight, w_query, w_keyval, w_attn_out, w_up,
            w_down, gains, final_gain, w_output,
        )
    )
    return pl.pallas_call(
        functools.partial(kernel, sizes),
        out_shape=jax.ShapeDtypeStruct(chain.shape, F32),
        in_specs=[hbm] * 15,
        out_specs=vmem,
        scratch_shapes=scratch,
        compiler_params=pltpu.CompilerParams(
            collective_id=0, has_side_effects=True, vmem_limit_bytes=48 * 1024 * 1024
        ),
    )(
        chain, start, noise, timesteps, rates, noise_scales, time_weight, w_query, w_keyval, w_attn_out,
        w_up, w_down, gains, final_gain, w_output,
    )


def solution(mesh):
    placed = (
        P(("groups", "step"), "person", None, None),
        P(("groups", "person"), None, None),
        P(("groups", "step"), "person", None, None),
        P(("groups", "step")),
        P(("groups", "step")),
        P(("groups", "step")),
    ) + (P(),) * 9
    return jax.shard_map(
        functools.partial(local, mesh.shape["person"], mesh.shape["step"]),
        mesh=mesh,
        in_specs=placed,
        out_specs=P(("groups", "step"), "person", None, None),
        check_vma=False,
    )
```
